32 devices in a mesh: groups: 2 (over x), branch: 2 (over core), sub: 8 (over z, y).
Axes of the slice: x: 2, y: 2, z: 4, core: 2. Of those that a mesh axis runs over, the one named last changes fastest.
Arguments:
- dispatch: float32 [128, 168, 2048], P(('groups', 'branch', 'sub')), parts along dimension 0, may hold values from 0 to 3
- multiplier: float32 [128, 48, 2048], P(('groups', 'branch', 'sub')), parts along dimension 0, may hold values from -3 to 3
- node_of: int32 [128], P(('groups', 'branch', 'sub')), parts along dimension 0, may hold values from 0 to 7, as said below
- prob_weight: int32 [128], P(('groups', 'branch', 'sub')), parts along dimension 0, may hold values from 1 to 16
- commitment: int32 [128, 168, 2048], P(('groups', 'branch', 'sub')), parts along dimension 0, may hold values 0 or 1
- zone_of: int32 [2048], replicated, may hold values from 0 to 31
- capacity: float32 [2048], replicated, may hold values from 0.5 to 4
- linear_cost: float32 [2048], replicated, may hold values from -0.5 to 1
- quad_cost: float32 [2048], replicated, may hold values from 0.5 to 2
- demand: float32 [128, 168, 32], P(('groups', 'branch', 'sub')), parts along dimension 0, may hold values from 19 to 64
Outputs:
- new_dispatch: float32 [128, 168, 2048], P(('groups', 'branch', 'sub')), parts along dimension 0
- new_multiplier: float32 [128, 48, 2048], P(('groups', 'branch', 'sub')), parts along dimension 0
- next_average: float32 [128, 48, 2048], P(('groups', 'branch', 'sub')), parts along dimension 0
- deviation: float32 [2], P('groups'), parts along dimension 0
The draws below stay inside these ranges and needn't reach their ends.
There are 2 independent parts, one for each index of `groups`. The reference program is written for one: setup_inputs(seed, part) draws one part's arguments, and reference() takes and returns one part's arrays. A program takes and returns all parts, laid end to end along the dimension named above; an argument that names none is the same for every part. Nothing has to cross between parts.
Inputs may be any that keep to these rules, and one draw needn't show every extreme that they name: `node_of`: within each aligned block of 32 scenarios (one day-one branch), every node number holds exactly 4 scenarios.
All inputs are finite; a program needn't handle non-finite values. No bound on the sum of `commitment` on one device may be relied on, other than what follows from the above.
Results may differ from the reference program's by a relative error of at most 0.0001.
Values sent between devices are 32-bit elements; how exact they have to be, the bound alone decides.
A program may use at most 128 MiB of HBM per device.

```python
import math
import jax
import jax.numpy as jnp
from jax import lax

G = 2048
HOURS = 168
DAY = 24
ZONES = 32
NODES_BR = 8
STEPS = 3
SECTION = 48
SCEN_BR = 32
SCEN = 64
N_BRANCH = 2


def branch_order(branch_key):
    return jax.random.permutation(branch_key, SCEN_BR)


def draw_node_of(key, part):
    branch_keys = jax.random.split(jax.random.fold_in(key, 7), SCEN // SCEN_BR)
    orders = jax.vmap(branch_order)(branch_keys)
    return (orders % NODES_BR).reshape(SCEN).astype(jnp.int32)


def touch_ends(entries, stream_key, least, top_value):
    longest = entries.shape.index(max(entries.shape))
    spots = []
    for shift in (0, 1):
        where = [jax.random.randint(jax.random.fold_in(stream_key, axis), (), 0, length) for axis, length in enumerate(entries.shape)]
        where[longest] = (where[longest] + shift) % entries.shape[longest]
        spots.append(tuple(where))
    return entries.at[spots[0]].set(least).at[spots[1]].set(top_value)


def steps_of(key, shape, pieces, least, largest):
    level, own = 1.0, jax.random.fold_in(key, 6)
    for position, shards_of in pieces:
        draws = jnp.exp(jax.random.uniform(jax.random.fold_in(own, position), (shards_of,), jnp.float32, least / len(pieces), largest / len(pieces)))
        level = level * jnp.repeat(draws, shape[position] // shards_of).reshape([-1 if axis == position else 1 for axis in range(len(shape))])
    return level


def gaussian(own_key, shape, scale, limit, pieces=(), kind=jnp.bfloat16):
    entries = scale * jax.random.normal(own_key, shape, jnp.float32)
    if pieces:
        entries = entries * steps_of(own_key, shape, pieces, -0.22, 0.18)
    return jnp.clip(entries, -limit, limit).astype(kind)


def setup_inputs(seed: int = 0, part: int = 0) -> dict:
    keys = jax.random.split(jax.random.key(seed), 11)
    part_keys = jax.random.split(jax.random.fold_in(keys[10], part), 11)
    return {
        "dispatch": jnp.clip(3.0 * jax.random.uniform(part_keys[0], (SCEN, HOURS, G), jnp.float32) ** steps_of(part_keys[0], (SCEN, HOURS, G), ((0, 16),), -0.2, 0.2), 0.0, 3.0),
        "multiplier": gaussian(part_keys[1], (SCEN, SECTION, G), 0.5, 3.0, ((0, 16),), jnp.float32),
        "node_of": draw_node_of(jax.random.fold_in(jax.random.fold_in(keys[10], part), 71), part),
        "prob_weight": touch_ends(jax.random.randint(part_keys[3], (SCEN,), 1, 17), jax.random.fold_in(part_keys[3], 1), 1, 16).astype(jnp.int32),
        "commitment": touch_ends((jax.random.randint(part_keys[4], (SCEN, HOURS, G), 0, 4) < 3).astype(jnp.int32), jax.random.fold_in(part_keys[4], 1), 0, 1),
        "zone_of": touch_ends(jax.random.randint(keys[5], (G,), 0, ZONES), jax.random.fold_in(keys[5], 1), 0, ZONES - 1).astype(jnp.int32),
        "capacity": jnp.clip(jnp.exp(jax.random.uniform(keys[6], (G,), jnp.float32, math.log(0.5), math.log(4.0))), 0.5, 4.0),
        "linear_cost": jnp.clip(jax.random.uniform(keys[7], (G,), jnp.float32, -0.5, 1.0), -0.5, 1.0),
        "quad_cost": jnp.clip(jnp.exp(jax.random.uniform(keys[8], (G,), jnp.float32, math.log(0.5), math.log(2.0))), 0.5, 2.0),
        "demand": jnp.clip(19.0 + 45.0 * jax.random.uniform(part_keys[9], (SCEN, HOURS, ZONES), jnp.float32) ** steps_of(part_keys[9], (SCEN, HOURS, ZONES), ((0, 16),), -0.2, 0.2), 19.0, 64.0),
    }


rho_value = 1.0
step_size = 0.3


def node_average(early_part, prob_weight, node_of):
    weighting = prob_weight.astype(jnp.float32)
    day_one = jnp.einsum("s,stg->tg", weighting, early_part[:, :DAY], precision=lax.Precision.HIGHEST)
    weight_sum = jnp.sum(weighting)
    root_mean = day_one / weight_sum
    node_key = (jnp.arange(SCEN, dtype=jnp.int32) // SCEN_BR) * NODES_BR + node_of
    member = (node_key[None, :] == jnp.arange(N_BRANCH * NODES_BR, dtype=jnp.int32)[:, None]).astype(jnp.float32)
    weighted = member * weighting[None, :]
    day_two = jnp.einsum("ks,stg->ktg", weighted, early_part[:, DAY:], precision=lax.Precision.HIGHEST)
    node_weight = jnp.sum(weighted, axis=1)
    node_mean = day_two / node_weight[:, None, None]
    assigned = node_mean[node_key]
    spread_root = jnp.broadcast_to(root_mean[None], (SCEN, DAY, G))
    return jnp.concatenate([spread_root, assigned], axis=1)


def reference(dispatch, multiplier, node_of, prob_weight, commitment, zone_of, capacity, linear_cost, quad_cost, demand):
    weighting = prob_weight.astype(jnp.float32)
    averages = node_average(dispatch[:, :SECTION], prob_weight, node_of)
    spread_gap = dispatch[:, :SECTION] - averages
    deviation = (jnp.sum(weighting[:, None, None] * spread_gap * spread_gap) / (jnp.sum(weighting) * SECTION * G))[None]
    new_multiplier = multiplier + rho_value * spread_gap
    zone_table = (zone_of[:, None] == jnp.arange(ZONES, dtype=jnp.int32)[None, :]).astype(jnp.float32)
    ceiling = capacity[None, None, :] * commitment.astype(jnp.float32)
    balance = ZONES / G
    current = dispatch
    for sweep in range(STEPS):
        zone_sum = jnp.einsum("stg,gz->stz", current, zone_table, precision=lax.Precision.HIGHEST)
        mismatch = zone_sum - demand
        feedback = jnp.einsum("stz,gz->stg", mismatch, zone_table, precision=lax.Precision.HIGHEST)
        gradient = linear_cost + quad_cost * current + balance * feedback
        hedged = gradient[:, :SECTION] + new_multiplier + rho_value * (current[:, :SECTION] - averages)
        gradient = jnp.concatenate([hedged, gradient[:, SECTION:]], axis=1)
        current = jnp.clip(current - step_size * gradient, 0.0, ceiling)
    next_average = node_average(current[:, :SECTION], prob_weight, node_of)
    return current, new_multiplier, next_average, deviation
```

```python
import functools

import jax
import jax.numpy as jnp
from jax import lax
from jax.experimental import pallas as pl
from jax.experimental.pallas import tpu as pltpu
from jax.sharding import PartitionSpec as P

DAY = 24
NODES_BR = 8
STEPS = 3
LANES = 128
EXTRA = 8

rho_value = 1.0
step_size = 0.3

MESH = pl.DeviceIdType.MESH


def kernel(
    n,
    zones_count,
    d_hbm,
    m_hbm,
    com_hbm,
    dem_ref,
    zone_ref,
    cap_ref,
    lin_ref,
    quad_ref,
    node_s,
    prob_s,
    out_d,
    out_m,
    out_a,
    out_dev,
    d_v,
    com_v,
    m_v,
    tab,
    tab_t,
    wt_all,
    recv2,
    back2,
    avg2,
    part1,
    pair1,
    recv1,
    back1,
    avg1,
    load_sem,
    store_sem,
    own_sem,
    wt_send,
    wt_recv,
    pair_send,
    pair_recv,
    send_sem,
    recv_sem,
):
    scen, hours, gens = d_v.shape
    section = m_v.shape[1]
    width = gens // n
    zones = zones_count
    balance = zones_count / gens
    me = lax.axis_index("sub")
    br = lax.axis_index("branch")
    day2 = pl.ds(DAY, DAY)

    def cols(i):
        return pl.ds(pl.multiple_of(i * width, LANES), width)

    loads = [
        pltpu.make_async_copy(d_hbm.at[:, pl.ds(0, section)], d_v.at[:, pl.ds(0, section)], load_sem.at[0]),
        pltpu.make_async_copy(
            d_hbm.at[:, pl.ds(section, hours - section)],
            d_v.at[:, pl.ds(section, hours - section)],
            load_sem.at[1],
        ),
        pltpu.make_async_copy(com_hbm, com_v, load_sem.at[2]),
        pltpu.make_async_copy(m_hbm, m_v, load_sem.at[3]),
    ]
    for load in loads:
        load.start()

    for j in range(scen):
        wt_all[me, j : j + 1, :] = jnp.full((1, LANES), prob_s[j].astype(jnp.float32), jnp.float32)
        wt_all[me, scen + j : scen + j + 1, :] = jnp.full(
            (1, LANES), node_s[j].astype(jnp.float32), jnp.float32
        )

    barrier = pltpu.get_barrier_semaphore()
    peers = [lax.rem(me + k, n) for k in range(1, n)]
    for peer in peers:
        pl.semaphore_signal(barrier, inc=1, device_id={"sub": peer}, device_id_type=MESH)
    pl.semaphore_signal(barrier, inc=1, device_id={"branch": 1 - br}, device_id_type=MESH)
    pl.semaphore_wait(barrier, n)

    def exchange(kind, src_of, dst):
        own = pltpu.make_async_copy(src_of(me), dst, own_sem.at[kind])
        own.start()
        copies = []
        for k, peer in enumerate(peers):
            copy = pltpu.make_async_remote_copy(
                src_ref=src_of(peer),
                dst_ref=dst,
                send_sem=send_sem.at[kind, k],
                recv_sem=recv_sem.at[kind, k],
                device_id={"sub": peer},
                device_id_type=MESH,
            )
            copy.start()
            copies.append(copy)
        return own, copies

    def arrive(flight):
        own, copies = flight
        own.wait()
        for copy in copies:
            copy.wait_recv()

    def left(flight):
        for copy in flight[1]:
            copy.wait_send()

    wt_copies = []
    for k, peer in enumerate(peers):
        copy = pltpu.make_async_remote_copy(
            src_ref=wt_all.at[me],
            dst_ref=wt_all.at[me],
            send_sem=wt_send.at[k],
            recv_sem=wt_recv.at[k],
            device_id={"sub": peer},
            device_id_type=MESH,
        )
        copy.start()
        wt_copies.append(copy)

    weights = [prob_s[j].astype(jnp.float32) for j in range(scen)]

    def pair(r):
        copy = pltpu.make_async_remote_copy(
            src_ref=part1.at[r],
            dst_ref=pair1.at[r],
            send_sem=pair_send.at[r],
            recv_sem=pair_recv.at[r],
            device_id={"branch": 1 - br},
            device_id_type=MESH,
        )
        copy.start()
        return copy

    def scatter2(r, src):
        return exchange(4 * r, lambda i: src.at[:, day2, cols(i)], recv2.at[r, me])

    def scatter1(r):
        return exchange(4 * r + 1, lambda i: pair1.at[r, :, cols(i)], recv1.at[r, me])

    def gather2(r):
        return exchange(4 * r + 2, lambda i: back2.at[r, i], avg2.at[r, :, :, cols(me)])

    def gather1(r):
        return exchange(4 * r + 3, lambda i: back1.at[r], avg1.at[r, :, cols(me)])

    def sum_day1(r):
        total = weights[0] * d_v[0, 0:DAY]
        for j in range(1, scen):
            total = total + weights[j] * d_v[j, 0:DAY]
        part1[r, 0:DAY] = total

    def mean1(r):
        total = recv1[r, 0]
        for q in range(1, n):
            total = total + recv1[r, q]
        if r == 0:
            weight = total[DAY : DAY + 1]
        else:
            weight = avg1[0, DAY : DAY + 1, 0:width]
        back1[r, 0:DAY] = total[0:DAY] / weight
        back1[r, DAY : DAY + EXTRA] = total[DAY : DAY + EXTRA]

    def mean2(r):
        for h in range(width // LANES):
            lane = slice(h * LANES, (h + 1) * LANES)

            def gather_sum(q, carry):
                sums, heft = list(carry[0]), list(carry[1])
                tile = wt_all[q]
                for j in range(scen):
                    x = recv2[r, q, j, :, lane]
                    w, node = tile[j : j + 1], tile[scen + j : scen + j + 1]
                    for key in range(NODES_BR):
                        part = jnp.where(node == float(key), w, 0.0)
                        sums[key] = sums[key] + part * x
                        heft[key] = heft[key] + part
                return tuple(sums), tuple(heft)

            zero = jnp.zeros((DAY, LANES), jnp.float32)
            row = jnp.zeros((1, LANES), jnp.float32)
            sums, heft = lax.fori_loop(
                0, n, gather_sum, ((zero,) * NODES_BR, (row,) * NODES_BR)
            )
            means = [sums[key] / heft[key] for key in range(NODES_BR)]

            def spread(q, carry):
                tile = wt_all[q]
                for j in range(scen):
                    node = tile[scen + j : scen + j + 1]
                    found = jnp.where(node == 0.0, 1.0, 0.0) * means[0]
                    for key in range(1, NODES_BR):
                        found = found + jnp.where(node == float(key), 1.0, 0.0) * means[key]
                    back2[r, q, j, :, lane] = found
                return carry

            lax.fori_loop(0, n, spread, 0)

    lane_id = lax.broadcasted_iota(jnp.int32, (1, LANES), 1)

    def sweeps(block, first, rows, base, slope):
        js, jn = block
        size = jn * rows
        view = (slice(js, js + jn), slice(first, first + rows))
        current = d_v[view].reshape(size, gens)
        demand = dem_ref[view].reshape(size, LANES)
        top = jnp.where(com_v[view].reshape(size, gens) > 0, cap_ref[...], 0.0)
        for sweep in range(STEPS):
            high = current.astype(jnp.bfloat16)
            low = (current - high.astype(jnp.float32)).astype(jnp.bfloat16)
            zone_sum = jnp.dot(high, tab[...], preferred_element_type=jnp.float32)
            zone_sum = zone_sum + jnp.dot(low, tab[...], preferred_element_type=jnp.float32)
            mismatch = (step_size * balance) * (zone_sum - demand)
            m_high = mismatch.astype(jnp.bfloat16).astype(jnp.float32)
            m_low = mismatch - m_high
            m_both = jnp.where(lane_id < zones, m_high, jnp.where(lane_id < 2 * zones, m_low, 0.0))
            feedback = jnp.dot(
                m_both.astype(jnp.bfloat16), tab_t[...], preferred_element_type=jnp.float32
            )
            current = jnp.minimum(jnp.maximum(slope * current - base - feedback, 0.0), top)
        d_v[view] = current.reshape(jn, rows, gens)

    lin = step_size * lin_ref[...]
    late_slope = 1.0 - step_size * quad_ref[...]
    early_slope = late_slope - step_size * rho_value

    def late(j):
        sweeps((j, 1), section, hours - section, lin, late_slope)
        copy = pltpu.make_async_copy(
            d_v.at[j, pl.ds(section, hours - section)],
            out_d.at[j, pl.ds(section, hours - section)],
            store_sem.at[j],
        )
        copy.start()
        return copy

    def early(first):
        pieces = []
        spread_sum = jnp.zeros((EXTRA, gens), jnp.float32)
        for j in range(scen):
            mean = avg1[0, 0:DAY] if first == 0 else avg2[0, j]
            gap = d_v[j, first : first + DAY] - mean
            changed = m_v[j, first : first + DAY] + rho_value * gap
            m_v[j, first : first + DAY] = changed
            square = (weights[j] * gap * gap).reshape(DAY // EXTRA, EXTRA, gens)
            spread_sum = spread_sum + jnp.sum(square, axis=0)
            pieces.append(lin + step_size * (changed - rho_value * mean))
        sweeps((0, scen), first, DAY, jnp.concatenate(pieces, axis=0), early_slope)
        return spread_sum

    flight2 = scatter2(0, d_hbm)
    loads[0].wait()
    sum_day1(0)
    part1[0, DAY : DAY + EXTRA] = jnp.full((EXTRA, gens), sum(weights), jnp.float32)
    copy = pair(0)
    ids = lax.broadcasted_iota(jnp.int32, (LANES, gens), 0) % zones
    one_hot = jnp.where(ids == zone_ref[...], 1.0, 0.0)
    tab_t[...] = one_hot.astype(jnp.bfloat16)
    tab[...] = one_hot.T.astype(jnp.bfloat16)
    copy.wait()
    pair1[0] = pair1[0] + part1[0]
    flight1 = scatter1(0)
    loads[1].wait()
    loads[2].wait()
    stores = [late(0)]
    arrive(flight1)
    mean1(0)
    back_flight1 = gather1(0)
    for copy in wt_copies:
        copy.wait()
    arrive(flight2)
    mean2(0)
    back_flight2 = gather2(0)
    loads[3].wait()
    stores.append(late(1))
    arrive(back_flight1)
    arrive(back_flight2)

    spread_two = early(DAY)
    second2 = scatter2(1, d_v)
    spread_one = early(0)
    sum_day1(1)
    part1[1, DAY : DAY + EXTRA] = spread_one + spread_two
    copy = pair(1)
    late_stores = [
        pltpu.make_async_copy(m_v, out_m, store_sem.at[scen]),
        pltpu.make_async_copy(
            d_v.at[:, pl.ds(0, section)], out_d.at[:, pl.ds(0, section)], store_sem.at[scen + 1]
        ),
    ]
    for store in late_stores:
        store.start()
    copy.wait()
    pair1[1] = pair1[1] + part1[1]
    second1 = scatter1(1)
    for j in range(2, scen - 1):
        stores.append(late(j))
    arrive(second1)
    mean1(1)
    back_second1 = gather1(1)
    arrive(second2)
    mean2(1)
    back_second2 = gather2(1)
    for j in range(scen - 1, scen):
        stores.append(late(j))
    arrive(back_second1)
    for j in range(scen):
        store = pltpu.make_async_copy(
            avg1.at[1, pl.ds(0, DAY)], out_a.at[j, pl.ds(0, DAY)], store_sem.at[scen + 2 + j]
        )
        store.start()
        stores.append(store)
    total = jnp.sum(avg1[1, DAY : DAY + EXTRA], keepdims=True)
    weight = avg1[0, DAY : DAY + 1, 0:1]
    out_dev[...] = jnp.broadcast_to(total / (weight * (section * gens)), out_dev.shape)
    arrive(back_second2)
    store = pltpu.make_async_copy(avg2.at[1], out_a.at[:, day2], store_sem.at[2 * scen + 2])
    store.start()
    stores.append(store)
    for flight in (
        flight1, flight2, back_flight1, back_flight2, second1, second2, back_second1, back_second2
    ):
        left(flight)
    for store in stores + late_stores:
        store.wait()


def shards(
    n,
    dispatch,
    multiplier,
    node_of,
    prob_weight,
    commitment,
    zone_of,
    capacity,
    linear_cost,
    quad_cost,
    demand,
):
    scen, hours, gens = dispatch.shape
    section = multiplier.shape[1]
    width = gens // n
    copies = LANES // demand.shape[2]
    wide = jnp.tile(demand, (1, 1, copies))
    any_spec = pl.BlockSpec(memory_space=pl.ANY)
    vmem = pl.BlockSpec(memory_space=pltpu.VMEM)
    smem = pl.BlockSpec(memory_space=pltpu.SMEM)
    f32 = jnp.float32
    dma = pltpu.SemaphoreType.DMA
    new_dispatch, new_multiplier, next_average, deviation = pl.pallas_call(
        functools.partial(kernel, n, demand.shape[2]),
        out_shape=(
            jax.ShapeDtypeStruct(dispatch.shape, f32),
            jax.ShapeDtypeStruct(multiplier.shape, f32),
            jax.ShapeDtypeStruct(multiplier.shape, f32),
            jax.ShapeDtypeStruct((8, LANES), f32),
        ),
        in_specs=[any_spec] * 3 + [vmem] * 5 + [smem] * 2,
        out_specs=(any_spec, any_spec, any_spec, vmem),
        scratch_shapes=[
            pltpu.VMEM((scen, hours, gens), f32),
            pltpu.VMEM((scen, hours, gens), jnp.int32),
            pltpu.VMEM((scen, section, gens), f32),
            pltpu.VMEM((gens, LANES), jnp.bfloat16),
            pltpu.VMEM((LANES, gens), jnp.bfloat16),
            pltpu.VMEM((n, 8, LANES), f32),
            pltpu.VMEM((2, n, scen, DAY, width), f32),
            pltpu.VMEM((2, n, scen, DAY, width), f32),
            pltpu.VMEM((2, scen, DAY, gens), f32),
            pltpu.VMEM((2, DAY + EXTRA, gens), f32),
            pltpu.VMEM((2, DAY + EXTRA, gens), f32),
            pltpu.VMEM((2, n, DAY + EXTRA, width), f32),
            pltpu.VMEM((2, DAY + EXTRA, width), f32),
            pltpu.VMEM((2, DAY + EXTRA, gens), f32),
            dma((4,)),
            dma((2 * scen + 3,)),
            dma((8,)),
            dma((n - 1,)),
            dma((n - 1,)),
            dma((2,)),
            dma((2,)),
            dma((8, n - 1)),
            dma((8, n - 1)),
        ],
        compiler_params=pltpu.CompilerParams(
            collective_id=0, has_side_effects=True, vmem_limit_bytes=56 * 1024 * 1024
        ),
    )(
        dispatch,
        multiplier,
        commitment,
        wide,
        zone_of[None],
        capacity[None],
        linear_cost[None],
        quad_cost[None],
        node_of,
        prob_weight,
    )
    return new_dispatch, new_multiplier, next_average, deviation[0, :1]


def solution(mesh):
    spread = ("groups", "branch", "sub")
    in_specs = (
        P(spread, None, None),
        P(spread, None, None),
        P(spread),
        P(spread),
        P(spread, None, None),
        P(),
        P(),
        P(),
        P(),
        P(spread, None, None),
    )
    out_specs = (P(spread, None, None), P(spread, None, None), P(spread, None, None), P("groups"))
    return jax.shard_map(
        functools.partial(shards, mesh.shape["sub"]),
        mesh=mesh,
        in_specs=in_specs,
        out_specs=out_specs,
        check_vma=False,
    )
```

```python
import functools

import jax
import jax.numpy as jnp
from jax import lax
from jax.experimental import pallas as pl
from jax.experimental.pallas import tpu as pltpu
from jax.sharding import PartitionSpec as P

DAY = 24
NODES_BR = 8
STEPS = 3
LANES = 128
EXTRA = 8

rho_value = 1.0
step_size = 0.3

MESH = pl.DeviceIdType.MESH


def kernel(
    n,
    zones,
    d_hbm,
    m_hbm,
    com_hbm,
    dem_ref,
    zone_ref,
    cap_ref,
    lin_ref,
    quad_ref,
    node_s,
    prob_s,
    out_d,
    out_m,
    out_a,
    out_dev,
    d_v,
    com_v,
    m_v,
    tab,
    tab_t,
    wt_all,
    dev_all,
    inv_node,
    swap2,
    own2,
    low2,
    high2,
    back2,
    avg2,
    swap1,
    own1,
    low1,
    high1,
    part1,
    pair1,
    avg1,
    load_sem,
    store_sem,
    tile_send,
    tile_recv,
    pair_send,
    pair_recv,
    swap_send,
    swap_recv,
    low_send,
    low_recv,
    high_send,
    high_recv,
    back_send,
    back_recv,
):
    scen, hours, gens = d_v.shape
    section = m_v.shape[1]
    chunks = gens // (2 * LANES)
    half = gens // 2
    balance = zones / gens
    me = lax.axis_index("sub")
    br = lax.axis_index("branch")
    side = lax.rem(me, 2)
    partner = me + 1 - 2 * side
    line = me // 2
    length = n // 2
    first_end, last_end = line == 0, line == length - 1
    middle = jnp.logical_and(line > 0, line < length - 1)
    place = br * n + me
    day2 = pl.ds(DAY, DAY)

    def lanes(owner, c):
        return pl.ds(pl.multiple_of(owner * half + c * LANES, LANES), LANES)

    def half_of(owner):
        return pl.ds(pl.multiple_of(owner * half, LANES), half)

    loads = [
        pltpu.make_async_copy(d_hbm.at[:, pl.ds(0, section)], d_v.at[:, pl.ds(0, section)], load_sem.at[0]),
        pltpu.make_async_copy(
            d_hbm.at[:, pl.ds(section, hours - section)],
            d_v.at[:, pl.ds(section, hours - section)],
            load_sem.at[1],
        ),
        pltpu.make_async_copy(com_hbm, com_v, load_sem.at[2]),
        pltpu.make_async_copy(m_hbm, m_v, load_sem.at[3]),
    ]
    for load in loads:
        load.start()

    for j in range(scen):
        wt_all[place, j : j + 1, :] = jnp.full((1, LANES), prob_s[j].astype(jnp.float32), jnp.float32)
        wt_all[place, scen + j : scen + j + 1, :] = jnp.full(
            (1, LANES), node_s[j].astype(jnp.float32), jnp.float32
        )

    others = [
        (lax.rem(br + flip, 2), lax.rem(me + k, n))
        for flip in range(2)
        for k in range(n)
        if flip or k
    ]
    barrier = pltpu.get_barrier_semaphore()
    for to_br, to_sub in others:
        pl.semaphore_signal(
            barrier, inc=1, device_id={"branch": to_br, "sub": to_sub}, device_id_type=MESH
        )
    pl.semaphore_wait(barrier, len(others))

    def remote(src, dst, send, recv, target):
        return pltpu.make_async_remote_copy(
            src_ref=src,
            dst_ref=dst,
            send_sem=send,
            recv_sem=recv,
            device_id=target,
            device_id_type=MESH,
        )

    def tiles(r, table):
        copies = []
        for k, (to_br, to_sub) in enumerate(others):
            copy = remote(
                table.at[place],
                table.at[place],
                tile_send.at[r, k],
                tile_recv.at[r, k],
                {"branch": to_br, "sub": to_sub},
            )
            copy.start()
            copies.append(copy)
        return copies

    weights = [prob_s[j].astype(jnp.float32) for j in range(scen)]

    def pair(r):
        copy = remote(
            part1.at[r], pair1.at[r], pair_send.at[r], pair_recv.at[r], {"branch": 1 - br}
        )
        copy.start()
        return copy

    def swap(r, c, src):
        if c < chunks:
            source, target = src.at[:, day2, lanes(1 - side, c)], swap2.at[r, c]
        else:
            source, target = pair1.at[r, :, half_of(1 - side)], swap1.at[r]
        return remote(source, target, swap_send.at[r, c], swap_recv.at[r, c], {"sub": partner})

    def buffers(r, c):
        if c < chunks:
            return own2.at[r, c], low2.at[r, c], high2.at[r, c]
        return own1.at[r], low1.at[r], high1.at[r]

    def upward(r, c):
        _, low, _ = buffers(r, c)
        return remote(low, low, low_send.at[r, c], low_recv.at[r, c], {"sub": lax.rem(me + 2, n)})

    def downward(r, c):
        own, _, high = buffers(r, c)
        return remote(
            own, high, high_send.at[r, c], high_recv.at[r, c], {"sub": lax.rem(me + n - 2, n)}
        )

    def back(r, c):
        if c < chunks:
            source, target = back2.at[r, c], avg2.at[r, :, :, lanes(side, c)]
        else:
            source = target = avg1.at[r, :, half_of(side)]
        return remote(source, target, back_send.at[r, c], back_recv.at[r, c], {"sub": partner})

    def masked(tile, j, key, value):
        return jnp.where(tile[scen + j : scen + j + 1] == float(key), value, 0.0)

    def begin(r, c, src):
        swap(r, c, src).wait_recv()
        own, low, high = buffers(r, c)
        if c < chunks:
            sums = [jnp.zeros((DAY, LANES), jnp.float32)] * NODES_BR
            for mine in (True, False):
                tile = wt_all[place if mine else br * n + partner]
                for j in range(scen):
                    own_x = d_v[j, DAY : 2 * DAY, lanes(side, c)] if mine else swap2[r, c, j]
                    for key in range(NODES_BR):
                        sums[key] = sums[key] + masked(tile, j, key, tile[j : j + 1]) * own_x
            for key in range(NODES_BR):
                own[key] = sums[key]
        else:
            own[...] = pair1[r, :, half_of(side)] + swap1[r]

        @pl.when(first_end)
        def _():
            low[...] = own[...]
            upward(r, c).start()

        @pl.when(last_end)
        def _():
            high[...] = jnp.zeros(high.shape, jnp.float32)
            downward(r, c).start()

    def finish(r, c):
        own, low, high = buffers(r, c)

        @pl.when(jnp.logical_not(first_end))
        def _():
            upward(r, c).wait_recv()
            low[...] = low[...] + own[...]

        @pl.when(middle)
        def _():
            upward(r, c).start()

        @pl.when(jnp.logical_not(last_end))
        def _():
            downward(r, c).wait_recv()

        @pl.when(middle)
        def _():
            own[...] = own[...] + high[...]
            downward(r, c).start()

        if c < chunks:
            means = [
                (low[key] + high[key]) * inv_node[key : key + 1] for key in range(NODES_BR)
            ]
            for which in range(2):
                tile = wt_all[place if which == 0 else br * n + partner]
                for j in range(scen):
                    found = masked(tile, j, 0, means[0])
                    for key in range(1, NODES_BR):
                        found = found + masked(tile, j, key, means[key])
                    if which == 0:
                        avg2[r, j, :, lanes(side, c)] = found
                    else:
                        back2[r, c, j] = found
        else:
            avg1[r, :, half_of(side)] = (low[...] + high[...]) * inv_node[NODES_BR, 0]
        back(r, c).start()

    def settle(r):
        for c in range(chunks + 1):
            swap(r, c, d_hbm if r == 0 else d_v).wait_send()
            back(r, c).wait_send()

            @pl.when(jnp.logical_not(last_end))
            def _():
                upward(r, c).wait_send()

            @pl.when(jnp.logical_not(first_end))
            def _():
                downward(r, c).wait_send()

    def chain(r, src):
        lag = 3
        for c in range(chunks + 1 + lag):
            if c < chunks + 1:
                begin(r, c, src)
            if c >= lag:
                finish(r, c - lag)

    def sum_day1(r):
        total = weights[0] * d_v[0, 0:DAY]
        for j in range(1, scen):
            total = total + weights[j] * d_v[j, 0:DAY]
        part1[r] = total

    lane_id = lax.broadcasted_iota(jnp.int32, (1, LANES), 1)

    def sweeps(block, first, rows, base, slope):
        js, jn = block
        size = jn * rows
        view = (slice(js, js + jn), slice(first, first + rows))
        current = d_v[view].reshape(size, gens)
        demand = dem_ref[view].reshape(size, LANES)
        top = jnp.where(com_v[view].reshape(size, gens) > 0, cap_ref[...], 0.0)
        for sweep in range(STEPS):
            high = current.astype(jnp.bfloat16)
            low = (current - high.astype(jnp.float32)).astype(jnp.bfloat16)
            zone_sum = jnp.dot(high, tab[...], preferred_element_type=jnp.float32)
            zone_sum = zone_sum + jnp.dot(low, tab[...], preferred_element_type=jnp.float32)
            mismatch = (step_size * balance) * (zone_sum - demand)
            m_high = mismatch.astype(jnp.bfloat16).astype(jnp.float32)
            m_low = mismatch - m_high
            m_both = jnp.where(lane_id < zones, m_high, jnp.where(lane_id < 2 * zones, m_low, 0.0))
            feedback = jnp.dot(
                m_both.astype(jnp.bfloat16), tab_t[...], preferred_element_type=jnp.float32
            )
            current = jnp.minimum(jnp.maximum(slope * current - base - feedback, 0.0), top)
        d_v[view] = current.reshape(jn, rows, gens)

    lin = step_size * lin_ref[...]
    late_slope = 1.0 - step_size * quad_ref[...]
    early_slope = late_slope - step_size * rho_value

    def late(j):
        sweeps((j, 1), section, hours - section, lin, late_slope)
        copy = pltpu.make_async_copy(
            d_v.at[j, pl.ds(section, hours - section)],
            out_d.at[j, pl.ds(section, hours - section)],
            store_sem.at[j],
        )
        copy.start()
        return copy

    def early(first):
        pieces = []
        spread_sum = jnp.zeros((EXTRA, gens), jnp.float32)
        for j in range(scen):
            mean = avg1[0] if first == 0 else avg2[0, j]
            gap = d_v[j, first : first + DAY] - mean
            changed = m_v[j, first : first + DAY] + rho_value * gap
            m_v[j, first : first + DAY] = changed
            square = (weights[j] * gap * gap).reshape(DAY // EXTRA, EXTRA, gens)
            spread_sum = spread_sum + jnp.sum(square, axis=0)
            pieces.append(lin + step_size * (changed - rho_value * mean))
        sweeps((0, scen), first, DAY, jnp.concatenate(pieces, axis=0), early_slope)
        return spread_sum

    for c in range(chunks):
        swap(0, c, d_hbm).start()
    wt_copies = tiles(0, wt_all)
    loads[0].wait()
    sum_day1(0)
    copy = pair(0)
    ids = lax.broadcasted_iota(jnp.int32, (LANES, gens), 0) % zones
    one_hot = jnp.where(ids == zone_ref[...], 1.0, 0.0)
    tab_t[...] = one_hot.astype(jnp.bfloat16)
    tab[...] = one_hot.T.astype(jnp.bfloat16)
    for tile_copy in wt_copies:
        tile_copy.wait()
    heft = [jnp.zeros((1, LANES), jnp.float32)] * NODES_BR
    for q in range(n):
        tile = wt_all[br * n + q]
        for j in range(scen):
            for key in range(NODES_BR):
                heft[key] = heft[key] + masked(tile, j, key, tile[j : j + 1])
    for key in range(NODES_BR):
        inv_node[key : key + 1] = 1.0 / heft[key]
    weight_sum = jnp.zeros((1, LANES), jnp.float32)
    for q in range(2 * n):
        for j in range(scen):
            weight_sum = weight_sum + wt_all[q, j : j + 1]
    inv_node[NODES_BR : NODES_BR + 1] = 1.0 / weight_sum
    copy.wait()
    pair1[0] = pair1[0] + part1[0]
    swap(0, chunks, d_hbm).start()
    chain(0, d_hbm)
    loads[1].wait()
    loads[2].wait()
    loads[3].wait()
    stores = [late(0)]
    for c in range(chunks + 1):
        back(0, c).wait_recv()

    spread_two = early(DAY)
    for c in range(chunks):
        swap(1, c, d_v).start()
    spread_one = early(0)
    sum_day1(1)
    copy = pair(1)
    spread_all = spread_one + spread_two
    spread_tile = spread_all[:, 0:LANES]
    for k in range(1, gens // LANES):
        spread_tile = spread_tile + spread_all[:, k * LANES : (k + 1) * LANES]
    dev_all[place] = spread_tile
    dev_copies = tiles(1, dev_all)
    late_stores = [
        pltpu.make_async_copy(m_v, out_m, store_sem.at[scen]),
        pltpu.make_async_copy(
            d_v.at[:, pl.ds(0, section)], out_d.at[:, pl.ds(0, section)], store_sem.at[scen + 1]
        ),
    ]
    for store in late_stores:
        store.start()
    copy.wait()
    pair1[1] = pair1[1] + part1[1]
    swap(1, chunks, d_v).start()
    chain(1, d_v)
    for j in range(1, scen):
        stores.append(late(j))
    for c in range(chunks + 1):
        back(1, c).wait_recv()
    for j in range(scen):
        store = pltpu.make_async_copy(
            avg1.at[1], out_a.at[j, pl.ds(0, DAY)], store_sem.at[scen + 2 + j]
        )
        store.start()
        stores.append(store)
    store = pltpu.make_async_copy(avg2.at[1], out_a.at[:, day2], store_sem.at[2 * scen + 2])
    store.start()
    stores.append(store)
    for copy in dev_copies:
        copy.wait()
    total = dev_all[0]
    for q in range(1, 2 * n):
        total = total + dev_all[q]
    total = jnp.sum(total, keepdims=True)
    out_dev[...] = jnp.broadcast_to(total / (weight_sum[:, 0:1] * (section * gens)), out_dev.shape)
    settle(0)
    settle(1)
    for store in stores + late_stores:
        store.wait()


def shards(
    n,
    dispatch,
    multiplier,
    node_of,
    prob_weight,
    commitment,
    zone_of,
    capacity,
    linear_cost,
    quad_cost,
    demand,
):
    scen, hours, gens = dispatch.shape
    section = multiplier.shape[1]
    chunks = gens // (2 * LANES)
    copies = LANES // demand.shape[2]
    wide = jnp.tile(demand, (1, 1, copies))
    any_spec = pl.BlockSpec(memory_space=pl.ANY)
    vmem = pl.BlockSpec(memory_space=pltpu.VMEM)
    smem = pl.BlockSpec(memory_space=pltpu.SMEM)
    f32 = jnp.float32
    dma = pltpu.SemaphoreType.DMA
    new_dispatch, new_multiplier, next_average, deviation = pl.pallas_call(
        functools.partial(kernel, n, demand.shape[2]),
        out_shape=(
            jax.ShapeDtypeStruct(dispatch.shape, f32),
            jax.ShapeDtypeStruct(multiplier.shape, f32),
            jax.ShapeDtypeStruct(multiplier.shape, f32),
            jax.ShapeDtypeStruct((8, LANES), f32),
        ),
        in_specs=[any_spec] * 3 + [vmem] * 5 + [smem] * 2,
        out_specs=(any_spec, any_spec, any_spec, vmem),
        scratch_shapes=[
            pltpu.VMEM((scen, hours, gens), f32),
            pltpu.VMEM((scen, hours, gens), jnp.int32),
            pltpu.VMEM((scen, section, gens), f32),
            pltpu.VMEM((gens, LANES), jnp.bfloat16),
            pltpu.VMEM((LANES, gens), jnp.bfloat16),
            pltpu.VMEM((2 * n, 8, LANES), f32),
            pltpu.VMEM((2 * n, 8, LANES), f32),
            pltpu.VMEM((2 * NODES_BR, LANES), f32),
            pltpu.VMEM((2, chunks, scen, DAY, LANES), f32),
            pltpu.VMEM((2, chunks, NODES_BR, DAY, LANES), f32),
            pltpu.VMEM((2, chunks, NODES_BR, DAY, LANES), f32),
            pltpu.VMEM((2, chunks, NODES_BR, DAY, LANES), f32),
            pltpu.VMEM((2, chunks, scen, DAY, LANES), f32),
            pltpu.VMEM((2, scen, DAY, gens), f32),
            pltpu.VMEM((2, DAY, gens // 2), f32),
            pltpu.VMEM((2, DAY, gens // 2), f32),
            pltpu.VMEM((2, DAY, gens // 2), f32),
            pltpu.VMEM((2, DAY, gens // 2), f32),
            pltpu.VMEM((2, DAY, gens), f32),
            pltpu.VMEM((2, DAY, gens), f32),
            pltpu.VMEM((2, DAY, gens), f32),
            dma((4,)),
            dma((2 * scen + 3,)),
            dma((2, 2 * n - 1)),
            dma((2, 2 * n - 1)),
            dma((2,)),
            dma((2,)),
        ]
        + [dma((2, chunks + 1))] * 8,
        compiler_params=pltpu.CompilerParams(
            collective_id=0, has_side_effects=True, vmem_limit_bytes=56 * 1024 * 1024
        ),
    )(
        dispatch,
        multiplier,
        commitment,
        wide,
        zone_of[None],
        capacity[None],
        linear_cost[None],
        quad_cost[None],
        node_of,
        prob_weight,
    )
    return new_dispatch, new_multiplier, next_average, deviation[0, :1]


def solution(mesh):
    spread = ("groups", "branch", "sub")
    in_specs = (
        P(spread, None, None),
        P(spread, None, None),
        P(spread),
        P(spread),
        P(spread, None, None),
        P(),
        P(),
        P(),
        P(),
        P(spread, None, None),
    )
    out_specs = (P(spread, None, None), P(spread, None, None), P(spread, None, None), P("groups"))
    return jax.shard_map(
        functools.partial(shards, mesh.shape["sub"]),
        mesh=mesh,
        in_specs=in_specs,
        out_specs=out_specs,
        check_vma=False,
    )
```

```python
import functools

import jax
import jax.numpy as jnp
from jax import lax
from jax.experimental import pallas as pl
from jax.experimental.pallas import tpu as pltpu
from jax.sharding import PartitionSpec as P

DAY = 24
NODES_BR = 8
STEPS = 3
LANES = 128
EXTRA = 8

rho_value = 1.0
step_size = 0.3

MESH = pl.DeviceIdType.MESH


def kernel(
    n,
    zones,
    d_hbm,
    m_hbm,
    com_hbm,
    dem_ref,
    zone_ref,
    cap_ref,
    lin_ref,
    quad_ref,
    node_s,
    prob_s,
    out_d,
    out_m,
    out_a,
    out_dev,
    d_v,
    com_v,
    m_v,
    tab,
    tab_t,
    wt_all,
    dev_all,
    inv_node,
    swap2,
    own2,
    low2,
    high2,
    rest2,
    back2,
    avg2,
    swap1,
    own1,
    low1,
    high1,
    rest1,
    part1,
    pair1,
    avg1,
    load_sem,
    store_sem,
    tile_send,
    tile_recv,
    pair_send,
    pair_recv,
    swap_send,
    swap_recv,
    low_send,
    low_recv,
    high_send,
    high_recv,
    back_send,
    back_recv,
):
    scen, hours, gens = d_v.shape
    section = m_v.shape[1]
    chunks = gens // (2 * LANES)
    half = gens // 2
    balance = zones / gens
    me = lax.axis_index("sub")
    br = lax.axis_index("branch")
    side = lax.rem(me, 2)
    partner = me + 1 - 2 * side
    line = me // 2
    length = n // 2
    first_end, last_end = line == 0, line == length - 1
    middle = jnp.logical_and(line > 0, line < length - 1)
    place = br * n + me
    day2 = pl.ds(DAY, DAY)

    def lanes(owner, c):
        return pl.ds(pl.multiple_of(owner * half + c * LANES, LANES), LANES)

    def half_of(owner):
        return pl.ds(pl.multiple_of(owner * half, LANES), half)

    loads = [
        pltpu.make_async_copy(d_hbm.at[:, pl.ds(0, section)], d_v.at[:, pl.ds(0, section)], load_sem.at[0]),
        pltpu.make_async_copy(
            d_hbm.at[:, pl.ds(section, hours - section)],
            d_v.at[:, pl.ds(section, hours - section)],
            load_sem.at[1],
        ),
        pltpu.make_async_copy(com_hbm, com_v, load_sem.at[2]),
        pltpu.make_async_copy(m_hbm, m_v, load_sem.at[3]),
    ]
    for load in loads:
        load.start()

    for j in range(scen):
        wt_all[place, j : j + 1, :] = jnp.full((1, LANES), prob_s[j].astype(jnp.float32), jnp.float32)
        wt_all[place, scen + j : scen + j + 1, :] = jnp.full(
            (1, LANES), node_s[j].astype(jnp.float32), jnp.float32
        )

    others = [
        (lax.rem(br + flip, 2), lax.rem(me + k, n))
        for flip in range(2)
        for k in range(n)
        if flip or k
    ]
    barrier = pltpu.get_barrier_semaphore()
    for to_br, to_sub in others:
        pl.semaphore_signal(
            barrier, inc=1, device_id={"branch": to_br, "sub": to_sub}, device_id_type=MESH
        )
    pl.semaphore_wait(barrier, len(others))

    def remote(src, dst, send, recv, target):
        return pltpu.make_async_remote_copy(
            src_ref=src,
            dst_ref=dst,
            send_sem=send,
            recv_sem=recv,
            device_id=target,
            device_id_type=MESH,
        )

    def tiles(r, table):
        copies = []
        for k, (to_br, to_sub) in enumerate(others):
            copy = remote(
                table.at[place],
                table.at[place],
                tile_send.at[r, k],
                tile_recv.at[r, k],
                {"branch": to_br, "sub": to_sub},
            )
            copy.start()
            copies.append(copy)
        return copies

    weights = [prob_s[j].astype(jnp.float32) for j in range(scen)]

    def pair(r):
        copy = remote(
            part1.at[r], pair1.at[r], pair_send.at[r], pair_recv.at[r], {"branch": 1 - br}
        )
        copy.start()
        return copy

    def swap(r, c, src):
        if c < chunks:
            source, target = src.at[:, day2, lanes(1 - side, c)], swap2.at[r, c]
        else:
            source, target = pair1.at[r, :, half_of(1 - side)], swap1.at[r]
        return remote(source, target, swap_send.at[r, c], swap_recv.at[r, c], {"sub": partner})

    def buffers(r, c):
        if c < chunks:
            return own2.at[r, c], low2.at[r, c], high2.at[r, c], rest2.at[r, c]
        return own1.at[r], low1.at[r], high1.at[r], rest1.at[r]

    def upward(r, c):
        _, low, _, _ = buffers(r, c)
        return remote(low, low, low_send.at[r, c], low_recv.at[r, c], {"sub": lax.rem(me + 2, n)})

    def downward(r, c):
        _, _, high, rest = buffers(r, c)
        return remote(
            rest, high, high_send.at[r, c], high_recv.at[r, c], {"sub": lax.rem(me + n - 2, n)}
        )

    def back(r, c):
        if c < chunks:
            source, target = back2.at[r, c], avg2.at[r, :, :, lanes(side, c)]
        else:
            source = target = avg1.at[r, :, half_of(side)]
        return remote(source, target, back_send.at[r, c], back_recv.at[r, c], {"sub": partner})

    def masked(tile, j, key, value):
        return jnp.where(tile[scen + j : scen + j + 1] == float(key), value, 0.0)

    def begin(r, c, src):
        swap(r, c, src).wait_recv()
        own, low, high, rest = buffers(r, c)
        if c < chunks:
            sums = [jnp.zeros((DAY, LANES), jnp.float32)] * NODES_BR
            for mine in (True, False):
                tile = wt_all[place if mine else br * n + partner]
                for j in range(scen):
                    own_x = d_v[j, DAY : 2 * DAY, lanes(side, c)] if mine else swap2[r, c, j]
                    for key in range(NODES_BR):
                        sums[key] = sums[key] + masked(tile, j, key, tile[j : j + 1]) * own_x
            for key in range(NODES_BR):
                own[key] = sums[key]
        else:
            own[...] = pair1[r, :, half_of(side)] + swap1[r]

        @pl.when(first_end)
        def _():
            low[...] = own[...]
            upward(r, c).start()

        @pl.when(last_end)
        def _():
            high[...] = jnp.zeros(high.shape, jnp.float32)
            rest[...] = own[...]
            downward(r, c).start()

    lower = line < length // 2
    upper = jnp.logical_not(lower)

    def go_up(r, c, when):
        own, low, _, _ = buffers(r, c)

        @pl.when(jnp.logical_and(when, jnp.logical_not(first_end)))
        def _():
            upward(r, c).wait_recv()
            low[...] = low[...] + own[...]

        @pl.when(jnp.logical_and(when, middle))
        def _():
            upward(r, c).start()

    def go_down(r, c, when):
        own, _, high, rest = buffers(r, c)

        @pl.when(jnp.logical_and(when, jnp.logical_not(last_end)))
        def _():
            downward(r, c).wait_recv()

        @pl.when(jnp.logical_and(when, middle))
        def _():
            rest[...] = own[...] + high[...]
            downward(r, c).start()

    def finish(r, c):
        own, low, high, _ = buffers(r, c)
        if c < chunks:
            means = [
                (low[key] + high[key]) * inv_node[key : key + 1] for key in range(NODES_BR)
            ]
            for which in range(2):
                tile = wt_all[place if which == 0 else br * n + partner]
                for j in range(scen):
                    found = masked(tile, j, 0, means[0])
                    for key in range(1, NODES_BR):
                        found = found + masked(tile, j, key, means[key])
                    if which == 0:
                        avg2[r, j, :, lanes(side, c)] = found
                    else:
                        back2[r, c, j] = found
        else:
            avg1[r, :, half_of(side)] = (low[...] + high[...]) * inv_node[NODES_BR, 0]
        back(r, c).start()

    def settle(r):
        for c in range(chunks + 1):
            swap(r, c, d_hbm if r == 0 else d_v).wait_send()
            back(r, c).wait_send()

            @pl.when(jnp.logical_not(last_end))
            def _():
                upward(r, c).wait_send()

            @pl.when(jnp.logical_not(first_end))
            def _():
                downward(r, c).wait_send()

    def chain(r, src, pieces):
        near, far = 1, 5
        for c in range(chunks + 1 + far):
            if c <= chunks:
                begin(r, c, src)
            if 0 <= c - near <= chunks:
                go_up(r, c - near, lower)
                go_down(r, c - near, upper)
            if c >= far:
                go_up(r, c - far, upper)
                go_down(r, c - far, lower)
                finish(r, c - far)
            if c >= 3 and c - 3 < len(pieces):
                pieces[c - 3]()

    def sum_day1(r):
        total = weights[0] * d_v[0, 0:DAY]
        for j in range(1, scen):
            total = total + weights[j] * d_v[j, 0:DAY]
        part1[r] = total

    lane_id = lax.broadcasted_iota(jnp.int32, (1, LANES), 1)

    def sweeps(block, first, rows, base, slope):
        js, jn = block
        size = jn * rows
        view = (slice(js, js + jn), slice(first, first + rows))
        current = d_v[view].reshape(size, gens)
        demand = dem_ref[view].reshape(size, LANES)
        top = jnp.where(com_v[view].reshape(size, gens) > 0, cap_ref[...], 0.0)
        for sweep in range(STEPS):
            high = current.astype(jnp.bfloat16)
            low = (current - high.astype(jnp.float32)).astype(jnp.bfloat16)
            zone_sum = jnp.dot(high, tab[...], preferred_element_type=jnp.float32)
            zone_sum = zone_sum + jnp.dot(low, tab[...], preferred_element_type=jnp.float32)
            mismatch = (step_size * balance) * (zone_sum - demand)
            m_high = mismatch.astype(jnp.bfloat16).astype(jnp.float32)
            m_low = mismatch - m_high
            m_both = jnp.where(lane_id < zones, m_high, jnp.where(lane_id < 2 * zones, m_low, 0.0))
            feedback = jnp.dot(
                m_both.astype(jnp.bfloat16), tab_t[...], preferred_element_type=jnp.float32
            )
            current = jnp.minimum(jnp.maximum(slope * current - base - feedback, 0.0), top)
        d_v[view] = current.reshape(jn, rows, gens)

    lin = step_size * lin_ref[...]
    late_slope = 1.0 - step_size * quad_ref[...]
    early_slope = late_slope - step_size * rho_value

    stores = []

    def late(k):
        j, part = k // 2, k % 2
        cut = section + (hours - section) // 16 * 8
        first, rows = (section, cut - section) if part == 0 else (cut, hours - cut)
        sweeps((j, 1), first, rows, lin, late_slope)
        store = pltpu.make_async_copy(
            d_v.at[j, pl.ds(first, rows)], out_d.at[j, pl.ds(first, rows)], store_sem.at[k]
        )
        store.start()
        stores.append(store)

    late_pieces = [functools.partial(late, k) for k in range(2 * scen)]

    def early(first):
        pieces = []
        spread_sum = jnp.zeros((EXTRA, gens), jnp.float32)
        for j in range(scen):
            mean = avg1[0] if first == 0 else avg2[0, j]
            gap = d_v[j, first : first + DAY] - mean
            changed = m_v[j, first : first + DAY] + rho_value * gap
            m_v[j, first : first + DAY] = changed
            square = (weights[j] * gap * gap).reshape(DAY // EXTRA, EXTRA, gens)
            spread_sum = spread_sum + jnp.sum(square, axis=0)
            pieces.append(lin + step_size * (changed - rho_value * mean))
        sweeps((0, scen), first, DAY, jnp.concatenate(pieces, axis=0), early_slope)
        return spread_sum

    for c in range(chunks):
        swap(0, c, d_hbm).start()
    wt_copies = tiles(0, wt_all)
    loads[0].wait()
    sum_day1(0)
    copy = pair(0)
    ids = lax.broadcasted_iota(jnp.int32, (LANES, gens), 0) % zones
    one_hot = jnp.where(ids == zone_ref[...], 1.0, 0.0)
    tab_t[...] = one_hot.astype(jnp.bfloat16)
    tab[...] = one_hot.T.astype(jnp.bfloat16)
    for tile_copy in wt_copies:
        tile_copy.wait()
    heft = [jnp.zeros((1, LANES), jnp.float32)] * NODES_BR
    for q in range(n):
        tile = wt_all[br * n + q]
        for j in range(scen):
            for key in range(NODES_BR):
                heft[key] = heft[key] + masked(tile, j, key, tile[j : j + 1])
    for key in range(NODES_BR):
        inv_node[key : key + 1] = 1.0 / heft[key]
    weight_sum = jnp.zeros((1, LANES), jnp.float32)
    for q in range(2 * n):
        for j in range(scen):
            weight_sum = weight_sum + wt_all[q, j : j + 1]
    inv_node[NODES_BR : NODES_BR + 1] = 1.0 / weight_sum
    copy.wait()
    pair1[0] = pair1[0] + part1[0]
    swap(0, chunks, d_hbm).start()
    for load in loads[1:]:
        load.wait()
    chain(0, d_hbm, late_pieces[:scen])
    for c in range(chunks + 1):
        back(0, c).wait_recv()

    spread_two = early(DAY)
    for c in range(chunks):
        swap(1, c, d_v).start()
    spread_one = early(0)
    sum_day1(1)
    copy = pair(1)
    spread_all = spread_one + spread_two
    spread_tile = spread_all[:, 0:LANES]
    for k in range(1, gens // LANES):
        spread_tile = spread_tile + spread_all[:, k * LANES : (k + 1) * LANES]
    dev_all[place] = spread_tile
    dev_copies = tiles(1, dev_all)
    late_stores = [
        pltpu.make_async_copy(m_v, out_m, store_sem.at[2 * scen]),
        pltpu.make_async_copy(
            d_v.at[:, pl.ds(0, section)], out_d.at[:, pl.ds(0, section)], store_sem.at[2 * scen + 1]
        ),
    ]
    for store in late_stores:
        store.start()
    copy.wait()
    pair1[1] = pair1[1] + part1[1]
    swap(1, chunks, d_v).start()
    chain(1, d_v, late_pieces[scen:])
    for c in range(chunks + 1):
        back(1, c).wait_recv()
    for j in range(scen):
        store = pltpu.make_async_copy(
            avg1.at[1], out_a.at[j, pl.ds(0, DAY)], store_sem.at[2 * scen + 2 + j]
        )
        store.start()
        stores.append(store)
    store = pltpu.make_async_copy(avg2.at[1], out_a.at[:, day2], store_sem.at[3 * scen + 2])
    store.start()
    stores.append(store)
    for copy in dev_copies:
        copy.wait()
    total = dev_all[0]
    for q in range(1, 2 * n):
        total = total + dev_all[q]
    total = jnp.sum(total, keepdims=True)
    out_dev[...] = jnp.broadcast_to(total / (weight_sum[:, 0:1] * (section * gens)), out_dev.shape)
    settle(0)
    settle(1)
    for store in stores + late_stores:
        store.wait()


def shards(
    n,
    dispatch,
    multiplier,
    node_of,
    prob_weight,
    commitment,
    zone_of,
    capacity,
    linear_cost,
    quad_cost,
    demand,
):
    scen, hours, gens = dispatch.shape
    section = multiplier.shape[1]
    chunks = gens // (2 * LANES)
    copies = LANES // demand.shape[2]
    wide = jnp.tile(demand, (1, 1, copies))
    any_spec = pl.BlockSpec(memory_space=pl.ANY)
    vmem = pl.BlockSpec(memory_space=pltpu.VMEM)
    smem = pl.BlockSpec(memory_space=pltpu.SMEM)
    f32 = jnp.float32
    dma = pltpu.SemaphoreType.DMA
    new_dispatch, new_multiplier, next_average, deviation = pl.pallas_call(
        functools.partial(kernel, n, demand.shape[2]),
        out_shape=(
            jax.ShapeDtypeStruct(dispatch.shape, f32),
            jax.ShapeDtypeStruct(multiplier.shape, f32),
            jax.ShapeDtypeStruct(multiplier.shape, f32),
            jax.ShapeDtypeStruct((8, LANES), f32),
        ),
        in_specs=[any_spec] * 3 + [vmem] * 5 + [smem] * 2,
        out_specs=(any_spec, any_spec, any_spec, vmem),
        scratch_shapes=[
            pltpu.VMEM((scen, hours, gens), f32),
            pltpu.VMEM((scen, hours, gens), jnp.int32),
            pltpu.VMEM((scen, section, gens), f32),
            pltpu.VMEM((gens, LANES), jnp.bfloat16),
            pltpu.VMEM((LANES, gens), jnp.bfloat16),
            pltpu.VMEM((2 * n, 8, LANES), f32),
            pltpu.VMEM((2 * n, 8, LANES), f32),
            pltpu.VMEM((2 * NODES_BR, LANES), f32),
            pltpu.VMEM((2, chunks, scen, DAY, LANES), f32),
            pltpu.VMEM((2, chunks, NODES_BR, DAY, LANES), f32),
            pltpu.VMEM((2, chunks, NODES_BR, DAY, LANES), f32),
            pltpu.VMEM((2, chunks, NODES_BR, DAY, LANES), f32),
            pltpu.VMEM((2, chunks, NODES_BR, DAY, LANES), f32),
            pltpu.VMEM((2, chunks, scen, DAY, LANES), f32),
            pltpu.VMEM((2, scen, DAY, gens), f32),
            pltpu.VMEM((2, DAY, gens // 2), f32),
            pltpu.VMEM((2, DAY, gens // 2), f32),
            pltpu.VMEM((2, DAY, gens // 2), f32),
            pltpu.VMEM((2, DAY, gens // 2), f32),
            pltpu.VMEM((2, DAY, gens // 2), f32),
            pltpu.VMEM((2, DAY, gens), f32),
            pltpu.VMEM((2, DAY, gens), f32),
            pltpu.VMEM((2, DAY, gens), f32),
            dma((4,)),
            dma((3 * scen + 3,)),
            dma((2, 2 * n - 1)),
            dma((2, 2 * n - 1)),
            dma((2,)),
            dma((2,)),
        ]
        + [dma((2, chunks + 1))] * 8,
        compiler_params=pltpu.CompilerParams(
            collective_id=0, has_side_effects=True, vmem_limit_bytes=56 * 1024 * 1024
        ),
    )(
        dispatch,
        multiplier,
        commitment,
        wide,
        zone_of[None],
        capacity[None],
        linear_cost[None],
        quad_cost[None],
        node_of,
        prob_weight,
    )
    return new_dispatch, new_multiplier, next_average, deviation[0, :1]


def solution(mesh):
    spread = ("groups", "branch", "sub")
    in_specs = (
        P(spread, None, None),
        P(spread, None, None),
        P(spread),
        P(spread),
        P(spread, None, None),
        P(),
        P(),
        P(),
        P(),
        P(spread, None, None),
    )
    out_specs = (P(spread, None, None), P(spread, None, None), P(spread, None, None), P("groups"))
    return jax.shard_map(
        functools.partial(shards, mesh.shape["sub"]),
        mesh=mesh,
        in_specs=in_specs,
        out_specs=out_specs,
        check_vma=False,
    )
```
